32 devices in a mesh: tm: 8 (over z, y), space: 4 (over x, core).
Axes of the slice: x: 2, y: 2, z: 4, core: 2. Of those that a mesh axis runs over, the one named last changes fastest.
Arguments:
- queries: bfloat16 [8, 16, 32, 768], P('tm', 'space')
- key_vectors: bfloat16 [8, 16, 32, 768], P('tm', 'space')
- values: bfloat16 [8, 16, 32, 768], P('tm', 'space'), may hold values from -6 to 6
- grad_out: bfloat16 [8, 16, 32, 768], P('tm', 'space'), may hold values from -6 to 6
- windows: int32 [2, 6], replicated, may hold values from 1 to 31, as said below
Outputs:
- attended: bfloat16 [8, 16, 32, 768], P('tm', 'space')
- grad_queries: bfloat16 [8, 16, 32, 768], P('tm', 'space')
- grad_keys: bfloat16 [8, 16, 32, 768], P('tm', 'space')
- value_gradient: bfloat16 [8, 16, 32, 768], P('tm', 'space')
The draws below stay inside these ranges and needn't reach their ends.
Inputs may be any that keep to these rules, and one draw needn't show every extreme that they name: windows[0, h] is 1 to 2 and some head has 2; windows[1, h] is a quarter of 32 or more and some head has 31.
All inputs are finite; a program needn't handle non-finite values.
Results may differ from the reference program's by a relative error of at most 0.025.
Values may be sent and summed in bfloat16 or wider, within the bound.
A program may use at most 64 MiB of HBM per device.

```python
import math
import jax
import jax.numpy as jnp
from jax import lax

HEADS = 6
HD = 128
R_DEV = 4
COLS = 32
FRAMES = 8
ROWS = 16
WIDTH = 768
N_TM = 8
N_SPACE = 4


def paired_fields(key):
    grid_shape = (FRAMES, ROWS, COLS, HEADS * HD)
    base_keys = jax.random.normal(jax.random.fold_in(key, 11), grid_shape, jnp.float32)
    return base_keys


def draw_queries(key, part):
    grid_shape = (FRAMES, ROWS, COLS, HEADS * HD)
    drawn_draw = jax.random.normal(jax.random.fold_in(key, 15), grid_shape, jnp.float32)
    return drawn_draw.astype(jnp.bfloat16)


def draw_key_vectors(key, part):
    base_keys = paired_fields(key)
    return base_keys.astype(jnp.bfloat16)


def draw_windows(key, part):
    head_ids = jnp.arange(HEADS, dtype=jnp.int32)
    row_reaches = jax.random.randint(jax.random.fold_in(key, 21), (HEADS,), 1, R_DEV // 2 + 1)
    col_reaches = jax.random.randint(jax.random.fold_in(key, 22), (HEADS,), max(1, COLS // 4), COLS)
    chosen = jax.random.randint(jax.random.fold_in(key, 23), (), 0, HEADS)
    second = (chosen + 1 + jax.random.randint(jax.random.fold_in(key, 24), (), 0, HEADS - 1)) % HEADS
    row_reaches = jnp.where(head_ids == chosen, R_DEV // 2, row_reaches)
    col_reaches = jnp.where(head_ids == second, COLS - 1, col_reaches)
    return jnp.stack([row_reaches, col_reaches]).astype(jnp.int32)


def block_levels(rng, extent, shards, least, largest):
    loudness, own = 1.0, jax.random.fold_in(rng, 6)
    for dim, shards_of in shards:
        steps = jnp.exp(jax.random.uniform(jax.random.fold_in(own, dim), (shards_of,), jnp.float32, least / len(shards), largest / len(shards)))
        loudness = loudness * jnp.repeat(steps, extent[dim] // shards_of).reshape([-1 if axis == dim else 1 for axis in range(len(extent))])
    return loudness


def noise(key, dims, spread, most, split=(), kind=jnp.bfloat16):
    values = jax.random.normal(key, dims, jnp.float32) * spread
    if len(split) > 0:
        values = block_levels(key, dims, split, -0.22, 0.18) * values
    return jnp.clip(values, min=-most, max=most).astype(kind)


def setup_inputs(seed: int = 0) -> dict:
    key_of = jax.random.split(jax.random.key(seed), 6)
    return {
        "queries": draw_queries(jax.random.fold_in(key_of[5], 71), 0),
        "key_vectors": draw_key_vectors(jax.random.fold_in(key_of[5], 71), 0),
        "values": noise(key_of[2], (FRAMES, ROWS, COLS, WIDTH), 1.0, 6.0, ((0, 8), (1, 4))),
        "grad_out": noise(key_of[3], (FRAMES, ROWS, COLS, WIDTH), 1.0, 6.0, ((0, 8), (1, 4))),
        "windows": draw_windows(jax.random.fold_in(key_of[5], 71), 0),
    }


masked_score = -1e+30

def window_mask(windows, frame_index, block_index, row_extent, row_count, col_count, frame_total, row_sum_total):
    query_count = row_count * col_count
    query_ids = jnp.arange(query_count, dtype=jnp.int32)
    query_row = query_ids // col_count
    query_col = query_ids % col_count
    near_rows = row_count + 2 * row_extent
    key_ids = jnp.arange(3 * near_rows * col_count, dtype=jnp.int32)
    key_frame = key_ids // (near_rows * col_count) - 1
    key_row = key_ids // col_count % near_rows - row_extent
    key_col = key_ids % col_count
    global_frame = frame_index + key_frame
    global_row = block_index * row_count + key_row
    inside = (global_frame >= 0) & (global_frame < frame_total) & (global_row >= 0) & (global_row < row_sum_total)
    row_gap = jnp.abs(query_row[:, None] - key_row[None, :])
    col_gap = jnp.abs(query_col[:, None] - key_col[None, :])
    return inside[None, None, :] & (row_gap[None] <= windows[0][:, None, None]) & (col_gap[None] <= windows[1][:, None, None])

def rounded(array):
    return lax.optimization_barrier(array.astype(jnp.bfloat16)).astype(jnp.float32)

def reference(queries, key_vectors, values, grad_out, windows):
    frame_total, row_sum_total, col_count, feature_count = queries.shape
    head_count = windows.shape[1]
    head_size = feature_count // head_count
    row_extent = R_DEV // 2
    near_rows = R_DEV + 2 * row_extent
    score_scale = 1.0 / math.sqrt(head_size)
    padding = ((1, 1), (row_extent, row_extent), (0, 0), (0, 0))
    keys_pad = jnp.pad(key_vectors.astype(jnp.float32), padding)
    values_pad = jnp.pad(values.astype(jnp.float32), padding)
    zero_index = jnp.zeros((), jnp.int32)
    nearby_window_shape = (3, near_rows, col_count, feature_count)
    local_shape = (1, R_DEV, col_count, feature_count)

    def loop_iteration(loop_carried, step_index):
        padded_key_gradient, padded_value_gradient = loop_carried
        frame_index = (step_index // N_SPACE).astype(jnp.int32)
        block_index = (step_index % N_SPACE).astype(jnp.int32)
        window_corner = (frame_index, (block_index * R_DEV).astype(jnp.int32), zero_index, zero_index)
        near_keys = lax.dynamic_slice(keys_pad, window_corner, nearby_window_shape).reshape(-1, head_count, head_size)
        near_values = lax.dynamic_slice(values_pad, window_corner, nearby_window_shape).reshape(-1, head_count, head_size)
        local_query = lax.dynamic_slice(queries, window_corner, local_shape).astype(jnp.float32).reshape(-1, head_count, head_size)
        local_grad = lax.dynamic_slice(grad_out, window_corner, local_shape).astype(jnp.float32).reshape(-1, head_count, head_size)
        in_window = window_mask(windows, frame_index, block_index, row_extent, R_DEV, col_count, frame_total, row_sum_total)
        scores = jnp.einsum('qhd,khd->hqk', local_query, near_keys) * score_scale
        scores = jnp.where(in_window, scores, masked_score)
        row_top = lax.optimization_barrier(jnp.max(scores, axis=2, keepdims=True))
        exp_total = lax.optimization_barrier(jnp.sum(jnp.where(in_window, jnp.exp(scores - row_top), 0.0), axis=2, keepdims=True))
        log_total = row_top + jnp.log(exp_total)
        soft_weights = jnp.where(in_window, jnp.exp(scores - log_total), 0.0)
        weights_low = rounded(soft_weights)
        attended = rounded(jnp.einsum('hqk,khd->qhd', weights_low, near_values))
        out_dot = jnp.einsum('qhd,qhd->hq', local_grad, attended)[:, :, None]
        grad_weights = jnp.einsum('qhd,khd->hqk', local_grad, near_values)
        grad_scores = rounded(soft_weights * (grad_weights - out_dot))
        grad_query = rounded(jnp.einsum('hqk,khd->qhd', grad_scores, near_keys) * score_scale)
        part_keys = (jnp.einsum('hqk,qhd->khd', grad_scores, local_query) * score_scale).reshape(nearby_window_shape)
        partial_value_rows = jnp.einsum('hqk,qhd->khd', weights_low, local_grad).reshape(nearby_window_shape)
        padded_key_gradient = lax.dynamic_update_slice(padded_key_gradient, lax.dynamic_slice(padded_key_gradient, window_corner, nearby_window_shape) + part_keys, window_corner)
        padded_value_gradient = lax.dynamic_update_slice(padded_value_gradient, lax.dynamic_slice(padded_value_gradient, window_corner, nearby_window_shape) + partial_value_rows, window_corner)
        output_rows = (attended.reshape(R_DEV, col_count, feature_count), grad_query.reshape(R_DEV, col_count, feature_count))
        return ((padded_key_gradient, padded_value_gradient), output_rows)
    start_position = (jnp.zeros(keys_pad.shape, jnp.float32), jnp.zeros(values_pad.shape, jnp.float32))
    (padded_key_gradient, padded_value_gradient), (attended_every_head, query_gradient_total) = lax.scan(loop_iteration, start_position, jnp.arange(N_TM * N_SPACE, dtype=jnp.int32))
    attended = attended_every_head.reshape(frame_total, row_sum_total, col_count, feature_count).astype(jnp.bfloat16)
    grad_queries = query_gradient_total.reshape(frame_total, row_sum_total, col_count, feature_count).astype(jnp.bfloat16)
    grad_keys = padded_key_gradient[1:-1, row_extent:row_extent + row_sum_total].astype(jnp.bfloat16)
    value_gradient = padded_value_gradient[1:-1, row_extent:row_extent + row_sum_total].astype(jnp.bfloat16)
    return (attended, grad_queries, grad_keys, value_gradient)
```

```python
import functools
import math

import jax
import jax.numpy as jnp
from jax import lax
from jax.experimental import pallas as pl
from jax.experimental.pallas import tpu as pltpu
from jax.sharding import PartitionSpec as P

masked_score = -1e30
MESH = pl.DeviceIdType.MESH
ORDER = (1, 2, 0, 3)


def dot_nt(a, b):
    return lax.dot_general(a, b, (((1,), (1,)), ((), ())), preferred_element_type=jnp.float32)


def dot_nn(a, b):
    return lax.dot_general(a, b, (((1,), (0,)), ((), ())), preferred_element_type=jnp.float32)


def kernel(
    sizes,
    win_ref,
    q_ref,
    k_ref,
    v_ref,
    g_ref,
    att_ref,
    gq_ref,
    gk_ref,
    gv_ref,
    near,
    stat_cols,
    st_main,
    st_down,
    st_up,
    load_sem,
    send_sem,
    recv_sem,
    stat_send,
    stat_recv,
):
    head_count, head_size, row_count, col_count, n_tm, n_space, chunks = sizes
    tokens = row_count * col_count
    half = tokens // 2
    width = head_count * head_size // chunks
    heads_in = width // head_size
    scale = 1.0 / math.sqrt(head_size)
    inputs = (q_ref, k_ref, v_ref, g_ref)
    tm, sp = lax.axis_index("tm"), lax.axis_index("space")
    side = lax.rem(tm, 2)
    pair = tm + 1 - 2 * side
    other = tm - 1 + 2 * side
    relay_to = tm + 2 - 4 * side
    relay_from = tm - 2 + 4 * side
    has_other = (other >= 0) & (other < n_tm)
    has_to = (relay_to >= 0) & (relay_to < n_tm)
    has_from = (relay_from >= 0) & (relay_from < n_tm)
    has_up = sp > 0
    has_down = sp < n_space - 1

    st_main[...] = jnp.zeros_like(st_main)
    st_down[...] = jnp.zeros_like(st_down)
    st_up[...] = jnp.zeros_like(st_up)

    barrier = pltpu.get_barrier_semaphore()

    def greet(cond, tm_to, sp_to):
        @pl.when(cond)
        def _():
            pl.semaphore_signal(barrier, inc=1, device_id=(tm_to, sp_to), device_id_type=MESH)

    pl.semaphore_signal(barrier, inc=1, device_id=(pair, sp), device_id_type=MESH)
    greet(has_to, relay_to, sp)
    greet(has_from, relay_from, sp)
    greet(has_up, tm, sp - 1)
    greet(has_down, tm, sp + 1)

    pieces = [(a, c) for group in ((1, 2), (0, 3)) for c in range(chunks) for a in group]

    def load(j):
        a, c = pieces[j]
        return pltpu.make_async_copy(
            inputs[a].at[:, c * width : (c + 1) * width],
            near.at[a, c, 0, 0:tokens, :],
            load_sem.at[j],
        )

    def remote(src, dst, j, i, device):
        return pltpu.make_async_remote_copy(
            src_ref=src,
            dst_ref=dst,
            send_sem=send_sem.at[j, i],
            recv_sem=recv_sem.at[j, i],
            device_id=device,
            device_id_type=MESH,
        )

    def to_pair(j):
        a, c = pieces[j]
        return remote(
            inputs[a].at[:, c * width : (c + 1) * width],
            near.at[a, c, 1, 0:tokens, :],
            j,
            0,
            (pair, sp),
        )

    def to_relay(j):
        a, c = pieces[j]
        return remote(
            near.at[a, c, 1, 0:tokens, :], near.at[a, c, 2, 0:tokens, :], j, 1, (relay_to, sp)
        )

    def to_up(j, slot):
        a, c = pieces[j]
        if slot == 0:
            src = inputs[a].at[0:half, c * width : (c + 1) * width]
        else:
            src = near.at[a, c, slot, 0:half, :]
        dst = near.at[a, c, slot, tokens : tokens + half, :]
        return remote(src, dst, j, 2 + slot, (tm, sp - 1))

    def to_down(j, slot):
        a, c = pieces[j]
        if slot == 0:
            src = inputs[a].at[half:tokens, c * width : (c + 1) * width]
        else:
            src = near.at[a, c, slot, half:tokens, :]
        dst = near.at[a, c, slot, tokens + half : 2 * tokens, :]
        return remote(src, dst, j, 5 + slot, (tm, sp + 1))

    def rows_out(j, slot):
        @pl.when(has_up)
        def _():
            to_up(j, slot).start()

        @pl.when(has_down)
        def _():
            to_down(j, slot).start()

    def pass_on(j):
        rows_out(j, 0)
        to_pair(j).wait_recv()

        @pl.when(has_to)
        def _():
            to_relay(j).start()

        rows_out(j, 1)

    def pass_other(j):
        @pl.when(has_other)
        def _():
            to_relay(j).wait_recv()
            rows_out(j, 2)

    def arrive(j):
        load(j).wait()

        @pl.when(has_down)
        def _():
            to_up(j, 0).wait_recv()
            to_up(j, 1).wait_recv()

        @pl.when(has_up)
        def _():
            to_down(j, 0).wait_recv()
            to_down(j, 1).wait_recv()

        @pl.when(has_down & has_other)
        def _():
            to_up(j, 2).wait_recv()

        @pl.when(has_up & has_other)
        def _():
            to_down(j, 2).wait_recv()

    count = len(pieces)
    for j in range(count):
        load(j).start()

    expected = (
        1
        + has_to.astype(jnp.int32)
        + has_from.astype(jnp.int32)
        + has_up.astype(jnp.int32)
        + has_down.astype(jnp.int32)
    )
    pl.semaphore_wait(barrier, expected)
    for j in range(count):
        to_pair(j).start()

    @pl.when(jnp.logical_not(has_other))
    def _():
        for a in range(4):
            for c in range(chunks):
                near[a, c, 2] = jnp.zeros((2 * tokens, width), near.dtype)

    @pl.when(jnp.logical_not(has_down))
    def _():
        for a in range(4):
            for c in range(chunks):
                near[a, c, :, tokens : tokens + half, :] = jnp.zeros((3, half, width), near.dtype)

    @pl.when(jnp.logical_not(has_up))
    def _():
        for a in range(4):
            for c in range(chunks):
                near[a, c, :, tokens + half : 2 * tokens, :] = jnp.zeros(
                    (3, half, width), near.dtype
                )

    own_id = lax.broadcasted_iota(jnp.int32, (tokens, 2 * tokens), 0)
    near_id = lax.broadcasted_iota(jnp.int32, (tokens, 2 * tokens), 1)
    own_row, own_col = own_id // col_count, own_id % col_count
    near_row, near_col = near_id // col_count, near_id % col_count
    upper = near_row >= row_count + row_count // 2
    near_row = jnp.where(upper, near_row - 2 * row_count, near_row)
    global_row = sp * row_count + near_row
    row_inside = (global_row >= 0) & (global_row < n_space * row_count)
    row_gap = jnp.where(row_inside, jnp.abs(own_row - near_row), 1 << 20)
    col_gap = jnp.abs(own_col - near_col)
    other_gap = jnp.where(has_other, 0, 1 << 20)

    def window(h):
        col_in = col_gap <= win_ref[1, h]
        here = (row_gap <= win_ref[0, h]) & col_in
        there = (row_gap + other_gap <= win_ref[0, h]) & col_in
        return jnp.concatenate([here, here, there], axis=1)

    lane = lax.broadcasted_iota(jnp.int32, (tokens, tokens), 1)

    def forward(c):
        for e in range(heads_in):
            h = c * heads_in + e
            cols = slice(e * head_size, (e + 1) * head_size)
            out_cols = slice(h * head_size, (h + 1) * head_size)
            query = near[0, c, 0, 0:tokens, cols]
            grad = near[3, c, 0, 0:tokens, cols]
            keys = near[1, c, :, :, cols].reshape(6 * tokens, head_size)
            vals = near[2, c, :, :, cols].reshape(6 * tokens, head_size)
            scores = jnp.where(window(h), dot_nt(query, keys) * scale, masked_score)
            top = jnp.max(scores, axis=1, keepdims=True)
            powers = jnp.exp(scores - top)
            total = jnp.sum(powers, axis=1, keepdims=True)
            soft = powers * (1.0 / total)
            attended = dot_nn(soft.astype(jnp.bfloat16), vals).astype(jnp.bfloat16)
            att_ref[:, out_cols] = attended
            out_dot = jnp.sum(
                grad.astype(jnp.float32) * attended.astype(jnp.float32), axis=1, keepdims=True
            )
            grad_scores = (soft * (dot_nt(grad, vals) - out_dot)).astype(jnp.bfloat16)
            gq_ref[:, out_cols] = (dot_nn(grad_scores, keys) * scale).astype(jnp.bfloat16)
            log_total = top + jnp.log(total)
            stats = jnp.where(lane == h, log_total, stat_cols[...])
            stat_cols[...] = jnp.where(lane == 8 + h, out_dot, stats)

    row_lane = lax.broadcasted_iota(jnp.int32, (1, tokens), 1)

    def stat_row(r):
        parts = []
        for slot in range(3):
            parts.append(st_main[slot, r : r + 1, :])
            parts.append(
                jnp.where(row_lane < half, st_down[slot, r : r + 1, :], st_up[slot, r : r + 1, :])
            )
        return jnp.concatenate(parts, axis=1)

    def backward(c):
        for e in range(heads_in):
            h = c * heads_in + e
            cols = slice(e * head_size, (e + 1) * head_size)
            out_cols = slice(h * head_size, (h + 1) * head_size)
            key = near[1, c, 0, 0:tokens, cols]
            val = near[2, c, 0, 0:tokens, cols]
            queries = near[0, c, :, :, cols].reshape(6 * tokens, head_size)
            grads = near[3, c, :, :, cols].reshape(6 * tokens, head_size)
            scores = dot_nt(key, queries) * scale - stat_row(h)
            soft = jnp.exp(jnp.where(window(h), scores, masked_score))
            gv_ref[:, out_cols] = dot_nn(soft.astype(jnp.bfloat16), grads).astype(jnp.bfloat16)
            grad_scores = (soft * (dot_nt(val, grads) - stat_row(8 + h))).astype(jnp.bfloat16)
            gk_ref[:, out_cols] = (dot_nn(grad_scores, queries) * scale).astype(jnp.bfloat16)

    def stat_copies():
        targets = [
            (None, st_main.at[1], (pair, sp)),
            (has_other, st_main.at[2], (other, sp)),
        ]
        for slot, (cond, frame) in enumerate(((None, tm), (None, pair), (has_other, other))):
            for at, there, cond_s in ((st_down, sp - 1, has_up), (st_up, sp + 1, has_down)):
                both = cond_s if cond is None else cond & cond_s
                targets.append((both, at.at[slot], (frame, there)))
        arrivals = [None, has_other]
        for cond in (None, None, has_other):
            for cond_s in (has_down, has_up):
                arrivals.append(cond_s if cond is None else cond & cond_s)
        found = []
        for i, (cond, dst, device) in enumerate(targets):
            copy = pltpu.make_async_remote_copy(
                src_ref=st_main.at[0],
                dst_ref=dst,
                send_sem=stat_send.at[i],
                recv_sem=stat_recv.at[i],
                device_id=device,
                device_id_type=MESH,
            )
            found.append((cond, arrivals[i], copy))
        return found

    def when(cond, action):
        if cond is None:
            action()
        else:
            pl.when(cond)(action)

    stat_cols[...] = jnp.zeros_like(stat_cols)
    per = 2
    lag = 1

    def own_ready(c):
        load(per * chunks + per * c).wait()
        load(per * chunks + per * c + 1).wait()

    def arrive_halo(j):
        @pl.when(has_down)
        def _():
            to_up(j, 0).wait_recv()
            to_up(j, 1).wait_recv()

        @pl.when(has_up)
        def _():
            to_down(j, 0).wait_recv()
            to_down(j, 1).wait_recv()

        @pl.when(has_down & has_other)
        def _():
            to_up(j, 2).wait_recv()

        @pl.when(has_up & has_other)
        def _():
            to_down(j, 2).wait_recv()

    def compute_forward(c):
        own_ready(c)
        for j in (per * c, per * c + 1):
            load(j).wait()
            arrive_halo(j)
        forward(c)

    def compute_backward(c):
        for j in (per * (chunks + c), per * (chunks + c) + 1):
            arrive_halo(j)
        backward(c)

    done_f = 0
    done_b = 0
    for j in range(count + lag):
        if j < count:
            pass_on(j)
        if j >= lag:
            pass_other(j - lag)
        if done_f < chunks and j >= per * (done_f + 1) + lag:
            compute_forward(done_f)
            done_f += 1
            if done_f == chunks:
                st_main[0] = stat_cols[...].T[0:16, :]
                for cond, _, copy in stat_copies():
                    when(cond, copy.start)
    for _, cond, copy in stat_copies():
        when(cond, copy.wait_recv)
    for c in range(chunks):
        compute_backward(c)

    for cond, _, copy in stat_copies():
        when(cond, copy.wait_send)
    for j in range(count):
        to_pair(j).wait_send()
        when(has_to, to_relay(j).wait_send)
        for slot in range(3):
            extra = has_other if slot == 2 else None
            when(has_up if extra is None else has_up & extra, to_up(j, slot).wait_send)
            when(has_down if extra is None else has_down & extra, to_down(j, slot).wait_send)


def on_device(queries, key_vectors, values, grad_out, windows):
    local_shape = queries.shape
    row_count, col_count, features = local_shape[1:]
    head_count = windows.shape[1]
    head_size = features // head_count
    tokens = row_count * col_count
    chunks = head_count // 2 if head_count % 2 == 0 else head_count
    width = features // chunks
    sizes = (
        head_count,
        head_size,
        row_count,
        col_count,
        lax.axis_size("tm"),
        lax.axis_size("space"),
        chunks,
    )
    flat = (tokens, features)
    count = 4 * chunks
    outs = pl.pallas_call(
        functools.partial(kernel, sizes),
        out_shape=[jax.ShapeDtypeStruct(flat, jnp.bfloat16)] * 4,
        in_specs=[pl.BlockSpec(memory_space=pltpu.SMEM)]
        + [pl.BlockSpec(memory_space=pl.ANY)] * 4,
        out_specs=[pl.BlockSpec(memory_space=pltpu.VMEM)] * 4,
        scratch_shapes=[
            pltpu.VMEM((4, chunks, 3, 2 * tokens, width), jnp.bfloat16),
            pltpu.VMEM((tokens, tokens), jnp.float32),
            pltpu.VMEM((3, 16, tokens), jnp.float32),
            pltpu.VMEM((3, 16, tokens), jnp.float32),
            pltpu.VMEM((3, 16, tokens), jnp.float32),
            pltpu.SemaphoreType.DMA((count,)),
            pltpu.SemaphoreType.DMA((count, 8)),
            pltpu.SemaphoreType.DMA((count, 8)),
            pltpu.SemaphoreType.DMA((8,)),
            pltpu.SemaphoreType.DMA((8,)),
        ],
        compiler_params=pltpu.CompilerParams(
            collective_id=0, has_side_effects=True, vmem_limit_bytes=40 * 1024 * 1024
        ),
    )(
        windows,
        queries.reshape(flat),
        key_vectors.reshape(flat),
        values.reshape(flat),
        grad_out.reshape(flat),
    )
    return tuple(out.reshape(local_shape) for out in outs)


def solution(mesh):
    spec = P("tm", "space", None, None)
    return jax.shard_map(
        on_device,
        mesh=mesh,
        in_specs=(spec, spec, spec, spec, P()),
        out_specs=(spec, spec, spec, spec),
        check_vma=False,
    )
```

```python
import functools
import math

import jax
import jax.numpy as jnp
from jax import lax
from jax.experimental import pallas as pl
from jax.experimental.pallas import tpu as pltpu
from jax.sharding import PartitionSpec as P

masked_score = -1e30
MESH = pl.DeviceIdType.MESH


def dot_nt(a, b):
    return lax.dot_general(a, b, (((1,), (1,)), ((), ())), preferred_element_type=jnp.float32)


def dot_nn(a, b):
    return lax.dot_general(a, b, (((1,), (0,)), ((), ())), preferred_element_type=jnp.float32)


def kernel(
    sizes,
    win_hbm,
    q_ref,
    k_ref,
    v_ref,
    g_ref,
    att_out,
    gq_out,
    gk_out,
    gv_out,
    win_ref,
    att_ref,
    gq_ref,
    gk_ref,
    gv_ref,
    near,
    stat_cols,
    st_main,
    st_down,
    st_up,
    load_sem,
    send_sem,
    recv_sem,
    stat_send,
    stat_recv,
    out_sem,
):
    head_count, head_size, row_count, col_count, n_tm, n_space, chunks = sizes
    tokens = row_count * col_count
    half = tokens // 2
    width = head_count * head_size // chunks
    heads_in = width // head_size
    scale = 1.0 / math.sqrt(head_size)
    inputs = (q_ref, k_ref, v_ref, g_ref)
    tm, sp = lax.axis_index("tm"), lax.axis_index("space")
    side = lax.rem(tm, 2)
    pair = tm + 1 - 2 * side
    other = tm - 1 + 2 * side
    relay_to = tm + 2 - 4 * side
    relay_from = tm - 2 + 4 * side
    has_other = (other >= 0) & (other < n_tm)
    has_to = (relay_to >= 0) & (relay_to < n_tm)
    has_from = (relay_from >= 0) & (relay_from < n_tm)
    has_up = sp > 0
    has_down = sp < n_space - 1

    st_main[...] = jnp.zeros_like(st_main)
    st_down[...] = jnp.zeros_like(st_down)
    st_up[...] = jnp.zeros_like(st_up)

    barrier = pltpu.get_barrier_semaphore()

    def greet(cond, tm_to, sp_to):
        @pl.when(cond)
        def _():
            pl.semaphore_signal(barrier, inc=1, device_id=(tm_to, sp_to), device_id_type=MESH)

    pl.semaphore_signal(barrier, inc=1, device_id=(pair, sp), device_id_type=MESH)
    greet(has_to, relay_to, sp)
    greet(has_from, relay_from, sp)
    greet(has_up, tm, sp - 1)
    greet(has_down, tm, sp + 1)

    pieces = [(a, c) for group in ((1, 2), (0, 3)) for c in range(chunks) for a in group]

    def load(j):
        a, c = pieces[j]
        return pltpu.make_async_copy(
            inputs[a].at[:, c * width : (c + 1) * width],
            near.at[a, c, 0, 0:tokens, :],
            load_sem.at[j],
        )

    def remote(src, dst, j, i, device):
        return pltpu.make_async_remote_copy(
            src_ref=src,
            dst_ref=dst,
            send_sem=send_sem.at[j, i],
            recv_sem=recv_sem.at[j, i],
            device_id=device,
            device_id_type=MESH,
        )

    def to_pair(j):
        a, c = pieces[j]
        return remote(
            inputs[a].at[:, c * width : (c + 1) * width],
            near.at[a, c, 1, 0:tokens, :],
            j,
            0,
            (pair, sp),
        )

    def to_relay(j):
        a, c = pieces[j]
        return remote(
            near.at[a, c, 1, 0:tokens, :], near.at[a, c, 2, 0:tokens, :], j, 1, (relay_to, sp)
        )

    def to_up(j, slot):
        a, c = pieces[j]
        if slot == 0:
            src = inputs[a].at[0:half, c * width : (c + 1) * width]
        else:
            src = near.at[a, c, slot, 0:half, :]
        dst = near.at[a, c, slot, tokens : tokens + half, :]
        return remote(src, dst, j, 2 + slot, (tm, sp - 1))

    def to_down(j, slot):
        a, c = pieces[j]
        if slot == 0:
            src = inputs[a].at[half:tokens, c * width : (c + 1) * width]
        else:
            src = near.at[a, c, slot, half:tokens, :]
        dst = near.at[a, c, slot, tokens + half : 2 * tokens, :]
        return remote(src, dst, j, 5 + slot, (tm, sp + 1))

    def rows_out(j, slot):
        @pl.when(has_up)
        def _():
            to_up(j, slot).start()

        @pl.when(has_down)
        def _():
            to_down(j, slot).start()

    def pass_on(j):
        rows_out(j, 0)
        to_pair(j).wait_recv()

        @pl.when(has_to)
        def _():
            to_relay(j).start()

        rows_out(j, 1)

    def pass_other(j):
        @pl.when(has_other)
        def _():
            to_relay(j).wait_recv()
            rows_out(j, 2)

    count = len(pieces)
    get_windows = pltpu.make_async_copy(win_hbm, win_ref, load_sem.at[count])
    get_windows.start()
    for j in range(count):
        load(j).start()

    expected = (
        1
        + has_to.astype(jnp.int32)
        + has_from.astype(jnp.int32)
        + has_up.astype(jnp.int32)
        + has_down.astype(jnp.int32)
    )
    pl.semaphore_wait(barrier, expected)
    for j in range(count):
        to_pair(j).start()

    @pl.when(jnp.logical_not(has_other))
    def _():
        for a in range(4):
            for c in range(chunks):
                near[a, c, 2] = jnp.zeros((2 * tokens, width), near.dtype)

    @pl.when(jnp.logical_not(has_down))
    def _():
        for a in range(4):
            for c in range(chunks):
                near[a, c, :, tokens : tokens + half, :] = jnp.zeros((3, half, width), near.dtype)

    @pl.when(jnp.logical_not(has_up))
    def _():
        for a in range(4):
            for c in range(chunks):
                near[a, c, :, tokens + half : 2 * tokens, :] = jnp.zeros(
                    (3, half, width), near.dtype
                )

    own_id = lax.broadcasted_iota(jnp.int32, (tokens, 2 * tokens), 0)
    near_id = lax.broadcasted_iota(jnp.int32, (tokens, 2 * tokens), 1)
    own_row, own_col = own_id // col_count, own_id % col_count
    near_row, near_col = near_id // col_count, near_id % col_count
    upper = near_row >= row_count + row_count // 2
    near_row = jnp.where(upper, near_row - 2 * row_count, near_row)
    global_row = sp * row_count + near_row
    row_inside = (global_row >= 0) & (global_row < n_space * row_count)
    row_gap = jnp.where(row_inside, jnp.abs(own_row - near_row), 1 << 20)
    col_gap = jnp.abs(own_col - near_col)
    other_gap = jnp.where(has_other, 0, 1 << 20)

    def window(h):
        col_in = col_gap <= win_ref[1, h]
        here = (row_gap <= win_ref[0, h]) & col_in
        there = (row_gap + other_gap <= win_ref[0, h]) & col_in
        return jnp.concatenate([here, here, there], axis=1)

    lane = lax.broadcasted_iota(jnp.int32, (tokens, tokens), 1)

    def forward(c):
        for e in range(heads_in):
            h = c * heads_in + e
            cols = slice(e * head_size, (e + 1) * head_size)
            out_cols = slice(h * head_size, (h + 1) * head_size)
            query = near[0, c, 0, 0:tokens, cols]
            grad = near[3, c, 0, 0:tokens, cols]
            keys = near[1, c, :, :, cols].reshape(6 * tokens, head_size)
            vals = near[2, c, :, :, cols].reshape(6 * tokens, head_size)
            scores = jnp.where(window(h), dot_nt(query, keys) * scale, masked_score)
            top = jnp.max(scores, axis=1, keepdims=True)
            powers = jnp.exp(scores - top)
            total = jnp.sum(powers, axis=1, keepdims=True)
            soft = powers * (1.0 / total)
            attended = dot_nn(soft.astype(jnp.bfloat16), vals).astype(jnp.bfloat16)
            att_ref[:, out_cols] = attended
            out_dot = jnp.sum(
                grad.astype(jnp.float32) * attended.astype(jnp.float32), axis=1, keepdims=True
            )
            grad_scores = (soft * (dot_nt(grad, vals) - out_dot)).astype(jnp.bfloat16)
            gq_ref[:, out_cols] = (dot_nn(grad_scores, keys) * scale).astype(jnp.bfloat16)
            log_total = top + jnp.log(total)
            stats = jnp.where(lane == h, log_total, stat_cols[...])
            stat_cols[...] = jnp.where(lane == 8 + h, out_dot, stats)

    row_lane = lax.broadcasted_iota(jnp.int32, (1, tokens), 1)

    def stat_row(r):
        parts = []
        for slot in range(3):
            parts.append(st_main[slot, r : r + 1, :])
            parts.append(
                jnp.where(row_lane < half, st_down[slot, r : r + 1, :], st_up[slot, r : r + 1, :])
            )
        return jnp.concatenate(parts, axis=1)

    def backward(c):
        for e in range(heads_in):
            h = c * heads_in + e
            cols = slice(e * head_size, (e + 1) * head_size)
            out_cols = slice(h * head_size, (h + 1) * head_size)
            key = near[1, c, 0, 0:tokens, cols]
            val = near[2, c, 0, 0:tokens, cols]
            queries = near[0, c, :, :, cols].reshape(6 * tokens, head_size)
            grads = near[3, c, :, :, cols].reshape(6 * tokens, head_size)
            scores = dot_nt(key, queries) * scale - stat_row(h)
            soft = jnp.exp(jnp.where(window(h), scores, masked_score))
            gv_ref[:, out_cols] = dot_nn(soft.astype(jnp.bfloat16), grads).astype(jnp.bfloat16)
            grad_scores = (soft * (dot_nt(val, grads) - stat_row(8 + h))).astype(jnp.bfloat16)
            gk_ref[:, out_cols] = (dot_nn(grad_scores, queries) * scale).astype(jnp.bfloat16)

    def stat_copies():
        targets = [
            (None, st_main.at[1], (pair, sp)),
            (has_other, st_main.at[2], (other, sp)),
        ]
        for slot, (cond, frame) in enumerate(((None, tm), (None, pair), (has_other, other))):
            for at, there, cond_s in ((st_down, sp - 1, has_up), (st_up, sp + 1, has_down)):
                both = cond_s if cond is None else cond & cond_s
                targets.append((both, at.at[slot], (frame, there)))
        arrivals = [None, has_other]
        for cond in (None, None, has_other):
            for cond_s in (has_down, has_up):
                arrivals.append(cond_s if cond is None else cond & cond_s)
        found = []
        for i, (cond, dst, device) in enumerate(targets):
            copy = pltpu.make_async_remote_copy(
                src_ref=st_main.at[0],
                dst_ref=dst,
                send_sem=stat_send.at[i],
                recv_sem=stat_recv.at[i],
                device_id=device,
                device_id_type=MESH,
            )
            found.append((cond, arrivals[i], copy))
        return found

    def when(cond, action):
        if cond is None:
            action()
        else:
            pl.when(cond)(action)

    stat_cols[...] = jnp.zeros_like(stat_cols)
    per = 2
    lag = 1

    def own_ready(c):
        load(per * chunks + per * c).wait()
        load(per * chunks + per * c + 1).wait()

    def arrive_halo(j):
        @pl.when(has_down)
        def _():
            to_up(j, 0).wait_recv()
            to_up(j, 1).wait_recv()

        @pl.when(has_up)
        def _():
            to_down(j, 0).wait_recv()
            to_down(j, 1).wait_recv()

        @pl.when(has_down & has_other)
        def _():
            to_up(j, 2).wait_recv()

        @pl.when(has_up & has_other)
        def _():
            to_down(j, 2).wait_recv()

    results = ((att_ref, att_out), (gq_ref, gq_out), (gk_ref, gk_out), (gv_ref, gv_out))

    def put(i, c):
        cols = slice(c * width, (c + 1) * width)
        return pltpu.make_async_copy(
            results[i][0].at[:, cols], results[i][1].at[:, cols], out_sem.at[i, c]
        )

    def compute_forward(c):
        if c == 0:
            get_windows.wait()
        own_ready(c)
        for j in (per * c, per * c + 1):
            load(j).wait()
            arrive_halo(j)
        forward(c)
        put(0, c).start()
        put(1, c).start()

    def compute_backward(c):
        for j in (per * (chunks + c), per * (chunks + c) + 1):
            arrive_halo(j)
        backward(c)
        put(2, c).start()
        put(3, c).start()

    done_f = 0
    done_b = 0
    for j in range(count + lag):
        if j < count:
            pass_on(j)
        if j >= lag:
            pass_other(j - lag)
        if done_f < chunks and j >= per * (done_f + 1) + lag:
            compute_forward(done_f)
            done_f += 1
            if done_f == chunks:
                st_main[0] = stat_cols[...].T[0:16, :]
                for cond, _, copy in stat_copies():
                    when(cond, copy.start)
    for _, cond, copy in stat_copies():
        when(cond, copy.wait_recv)
    for c in range(chunks):
        compute_backward(c)

    for cond, _, copy in stat_copies():
        when(cond, copy.wait_send)
    for j in range(count):
        to_pair(j).wait_send()
        when(has_to, to_relay(j).wait_send)
        for slot in range(3):
            extra = has_other if slot == 2 else None
            when(has_up if extra is None else has_up & extra, to_up(j, slot).wait_send)
            when(has_down if extra is None else has_down & extra, to_down(j, slot).wait_send)
    for i in range(4):
        for c in range(chunks):
            put(i, c).wait()


def put_out(*refs):
    sources, targets, held, come, go = refs[:4], refs[4:8], refs[8], refs[9], refs[10]
    ins = [pltpu.make_async_copy(sources[i], held.at[i], come.at[i]) for i in range(4)]
    outs = [pltpu.make_async_copy(held.at[i], targets[i], go.at[i]) for i in range(4)]
    for copy in ins:
        copy.start()
    for i in range(4):
        ins[i].wait()
        outs[i].start()
    for copy in outs:
        copy.wait()


def on_device(queries, key_vectors, values, grad_out, windows):
    local_shape = queries.shape
    row_count, col_count, features = local_shape[1:]
    head_count = windows.shape[1]
    head_size = features // head_count
    tokens = row_count * col_count
    chunks = head_count // 2 if head_count % 2 == 0 else head_count
    width = features // chunks
    sizes = (
        head_count,
        head_size,
        row_count,
        col_count,
        lax.axis_size("tm"),
        lax.axis_size("space"),
        chunks,
    )
    flat = (tokens, features)
    count = 4 * chunks
    outs = pl.pallas_call(
        functools.partial(kernel, sizes),
        out_shape=[jax.ShapeDtypeStruct(flat, jnp.bfloat16)] * 4,
        in_specs=[pl.BlockSpec(memory_space=pl.ANY)] * 5,
        out_specs=[pl.BlockSpec(memory_space=pl.ANY)] * 4,
        scratch_shapes=[
            pltpu.SMEM((2, head_count), jnp.int32),
            pltpu.VMEM(flat, jnp.bfloat16),
            pltpu.VMEM(flat, jnp.bfloat16),
            pltpu.VMEM(flat, jnp.bfloat16),
            pltpu.VMEM(flat, jnp.bfloat16),
            pltpu.VMEM((4, chunks, 3, 2 * tokens, width), jnp.bfloat16),
            pltpu.VMEM((tokens, tokens), jnp.float32),
            pltpu.VMEM((3, 16, tokens), jnp.float32),
            pltpu.VMEM((3, 16, tokens), jnp.float32),
            pltpu.VMEM((3, 16, tokens), jnp.float32),
            pltpu.SemaphoreType.DMA((count + 1,)),
            pltpu.SemaphoreType.DMA((count, 8)),
            pltpu.SemaphoreType.DMA((count, 8)),
            pltpu.SemaphoreType.DMA((8,)),
            pltpu.SemaphoreType.DMA((8,)),
            pltpu.SemaphoreType.DMA((4, chunks)),
        ],
        compiler_params=pltpu.CompilerParams(
            collective_id=0, has_side_effects=True, vmem_limit_bytes=63_000_000
        ),
    )(
        windows,
        queries.reshape(flat),
        key_vectors.reshape(flat),
        values.reshape(flat),
        grad_out.reshape(flat),
    )
    outs = pl.pallas_call(
        put_out,
        out_shape=[jax.ShapeDtypeStruct(flat, jnp.bfloat16)] * 4,
        in_specs=[pl.BlockSpec(memory_space=pl.ANY)] * 4,
        out_specs=[pl.BlockSpec(memory_space=pl.ANY)] * 4,
        scratch_shapes=[
            pltpu.VMEM((4,) + flat, jnp.bfloat16),
            pltpu.SemaphoreType.DMA((4,)),
            pltpu.SemaphoreType.DMA((4,)),
        ],
        compiler_params=pltpu.CompilerParams(vmem_limit_bytes=63_000_000),
    )(*outs)
    return tuple(out.reshape(local_shape) for out in outs)


def solution(mesh):
    spec = P("tm", "space", None, None)
    return jax.shard_map(
        on_device,
        mesh=mesh,
        in_specs=(spec, spec, spec, spec, P()),
        out_specs=(spec, spec, spec, spec),
        check_vma=False,
    )
```

```python
import functools
import math

import jax
import jax.numpy as jnp
from jax import lax
from jax.experimental import pallas as pl
from jax.experimental.pallas import tpu as pltpu
from jax.sharding import PartitionSpec as P

masked_score = -1e30
MESH = pl.DeviceIdType.MESH


def dot_nt(a, b):
    return lax.dot_general(a, b, (((1,), (1,)), ((), ())), preferred_element_type=jnp.float32)


def dot_nn(a, b):
    return lax.dot_general(a, b, (((1,), (0,)), ((), ())), preferred_element_type=jnp.float32)


def kernel(
    sizes,
    win_hbm,
    q_ref,
    k_ref,
    v_ref,
    g_ref,
    att_out,
    gq_out,
    gk_out,
    gv_out,
    win_ref,
    att_ref,
    gq_ref,
    gk_ref,
    gv_ref,
    near,
    stat_cols,
    st_main,
    st_down,
    st_up,
    load_sem,
    send_sem,
    recv_sem,
    stat_send,
    stat_recv,
    out_sem,
):
    head_count, head_size, row_count, col_count, n_tm, n_space = sizes
    tokens = row_count * col_count
    half = tokens // 2
    scale = 1.0 / math.sqrt(head_size)
    tm, sp = lax.axis_index("tm"), lax.axis_index("space")
    side = lax.rem(tm, 2)
    pair = tm + 1 - 2 * side
    other = tm - 1 + 2 * side
    relay_to = tm + 2 - 4 * side
    relay_from = tm - 2 + 4 * side
    has_other = (other >= 0) & (other < n_tm)
    has_to = (relay_to >= 0) & (relay_to < n_tm)
    has_from = (relay_from >= 0) & (relay_from < n_tm)
    has_up = sp > 0
    has_down = sp < n_space - 1

    st_main[...] = jnp.zeros_like(st_main)
    st_down[...] = jnp.zeros_like(st_down)
    st_up[...] = jnp.zeros_like(st_up)

    barrier = pltpu.get_barrier_semaphore()

    def greet(cond, tm_to, sp_to):
        @pl.when(cond)
        def _():
            pl.semaphore_signal(barrier, inc=1, device_id=(tm_to, sp_to), device_id_type=MESH)

    pl.semaphore_signal(barrier, inc=1, device_id=(pair, sp), device_id_type=MESH)
    greet(has_to, relay_to, sp)
    greet(has_from, relay_from, sp)
    greet(has_up, tm, sp - 1)
    greet(has_down, tm, sp + 1)

    near_arrays = ((k_ref, v_ref), (q_ref, g_ref))
    pieces = [(phase, h) for phase in range(2) for h in range(head_count)]
    count = len(pieces)

    def block(j, slot, start, size):
        phase, h = pieces[j]
        return near.at[phase, h, :, slot, start : start + size, :]

    def source(j, a):
        phase, h = pieces[j]
        return near_arrays[phase][a].at[:, h * head_size : (h + 1) * head_size]

    def load(j, a):
        phase, h = pieces[j]
        return pltpu.make_async_copy(
            source(j, a), near.at[phase, h, a, 0, 0:tokens, :], load_sem.at[j]
        )

    def load_wait(j):
        whole = block(j, 0, 0, tokens)
        pltpu.make_async_copy(whole, whole, load_sem.at[j]).wait()

    def remote(src, dst, send, recv, device):
        return pltpu.make_async_remote_copy(
            src_ref=src,
            dst_ref=dst,
            send_sem=send,
            recv_sem=recv,
            device_id=device,
            device_id_type=MESH,
        )

    def to_pair(j, a):
        phase, h = pieces[j]
        return remote(
            source(j, a),
            near.at[phase, h, a, 1, 0:tokens, :],
            send_sem.at[0],
            recv_sem.at[j, 0],
            (pair, sp),
        )

    def both_pair(j):
        whole = block(j, 1, 0, tokens)
        return remote(whole, whole, send_sem.at[0], recv_sem.at[j, 0], (pair, sp))

    def to_relay(j):
        return remote(
            block(j, 1, 0, tokens),
            block(j, 2, 0, tokens),
            send_sem.at[1],
            recv_sem.at[j, 1],
            (relay_to, sp),
        )

    def to_up(j, slot, size=None):
        slots = slot if size is None else slice(slot, slot + size)
        late = 1 if slot == 2 else 0
        return remote(
            block(j, slots, 0, half),
            block(j, slots, tokens, half),
            send_sem.at[2 + late],
            recv_sem.at[j, 2 + late],
            (tm, sp - 1),
        )

    def to_down(j, slot, size=None):
        slots = slot if size is None else slice(slot, slot + size)
        late = 1 if slot == 2 else 0
        return remote(
            block(j, slots, half, half),
            block(j, slots, tokens + half, half),
            send_sem.at[4 + late],
            recv_sem.at[j, 4 + late],
            (tm, sp + 1),
        )

    def rows_out(j, slot):
        @pl.when(has_up)
        def _():
            to_up(j, slot).start()

        @pl.when(has_down)
        def _():
            to_down(j, slot).start()

    def pass_on(j):
        if pieces[j][0] == 0:
            load_wait(j)
        rows_out(j, 0)
        both_pair(j).wait_recv()

        @pl.when(has_to)
        def _():
            to_relay(j).start()

        rows_out(j, 1)

    def pass_other(j):
        @pl.when(has_other)
        def _():
            to_relay(j).wait_recv()
            rows_out(j, 2)

    def arrive_halo(j):
        @pl.when(has_down)
        def _():
            to_up(j, 0, 2).wait_recv()

        @pl.when(has_up)
        def _():
            to_down(j, 0, 2).wait_recv()

        @pl.when(has_down & has_other)
        def _():
            to_up(j, 2).wait_recv()

        @pl.when(has_up & has_other)
        def _():
            to_down(j, 2).wait_recv()

    get_windows = pltpu.make_async_copy(win_hbm, win_ref, load_sem.at[count])
    get_windows.start()
    for j in range(count):
        for a in range(2):
            load(j, a).start()

    expected = (
        1
        + has_to.astype(jnp.int32)
        + has_from.astype(jnp.int32)
        + has_up.astype(jnp.int32)
        + has_down.astype(jnp.int32)
    )
    pl.semaphore_wait(barrier, expected)
    for j in range(count):
        for a in range(2):
            to_pair(j, a).start()

    @pl.when(jnp.logical_not(has_other))
    def _():
        for phase, h in pieces:
            near[phase, h, :, 2] = jnp.zeros((2, 2 * tokens, head_size), near.dtype)

    @pl.when(jnp.logical_not(has_down))
    def _():
        for phase, h in pieces:
            near[phase, h, :, :, tokens : tokens + half, :] = jnp.zeros(
                (2, 3, half, head_size), near.dtype
            )

    @pl.when(jnp.logical_not(has_up))
    def _():
        for phase, h in pieces:
            near[phase, h, :, :, tokens + half : 2 * tokens, :] = jnp.zeros(
                (2, 3, half, head_size), near.dtype
            )

    own_id = lax.broadcasted_iota(jnp.int32, (tokens, 2 * tokens), 0)
    near_id = lax.broadcasted_iota(jnp.int32, (tokens, 2 * tokens), 1)
    own_row, own_col = own_id // col_count, own_id % col_count
    near_row, near_col = near_id // col_count, near_id % col_count
    upper = near_row >= row_count + row_count // 2
    near_row = jnp.where(upper, near_row - 2 * row_count, near_row)
    global_row = sp * row_count + near_row
    row_inside = (global_row >= 0) & (global_row < n_space * row_count)
    row_gap = jnp.where(row_inside, jnp.abs(own_row - near_row), 1 << 20)
    col_gap = jnp.abs(own_col - near_col)
    other_gap = jnp.where(has_other, 0, 1 << 20)

    def window(h):
        col_in = col_gap <= win_ref[1, h]
        here = (row_gap <= win_ref[0, h]) & col_in
        there = (row_gap + other_gap <= win_ref[0, h]) & col_in
        return jnp.concatenate([here, here, there], axis=1)

    lane = lax.broadcasted_iota(jnp.int32, (tokens, tokens), 1)

    def forward(h):
        out_cols = slice(h * head_size, (h + 1) * head_size)
        query = near[1, h, 0, 0, 0:tokens, :]
        grad = near[1, h, 1, 0, 0:tokens, :]
        keys = near[0, h, 0].reshape(6 * tokens, head_size)
        vals = near[0, h, 1].reshape(6 * tokens, head_size)
        scores = jnp.where(window(h), dot_nt(query, keys) * scale, masked_score)
        top = jnp.max(scores, axis=1, keepdims=True)
        powers = jnp.exp(scores - top)
        total = jnp.sum(powers, axis=1, keepdims=True)
        soft = powers * (1.0 / total)
        attended = dot_nn(soft.astype(jnp.bfloat16), vals).astype(jnp.bfloat16)
        att_ref[:, out_cols] = attended
        out_dot = jnp.sum(
            grad.astype(jnp.float32) * attended.astype(jnp.float32), axis=1, keepdims=True
        )
        grad_scores = (soft * (dot_nt(grad, vals) - out_dot)).astype(jnp.bfloat16)
        gq_ref[:, out_cols] = (dot_nn(grad_scores, keys) * scale).astype(jnp.bfloat16)
        log_total = top + jnp.log(total)
        stats = jnp.where(lane == h, log_total, stat_cols[...])
        stat_cols[...] = jnp.where(lane == 8 + h, out_dot, stats)

    row_lane = lax.broadcasted_iota(jnp.int32, (1, tokens), 1)

    def stat_row(r):
        parts = []
        for slot in range(3):
            parts.append(st_main[slot, r : r + 1, :])
            parts.append(
                jnp.where(row_lane < half, st_down[slot, r : r + 1, :], st_up[slot, r : r + 1, :])
            )
        return jnp.concatenate(parts, axis=1)

    def backward(h):
        out_cols = slice(h * head_size, (h + 1) * head_size)
        key = near[0, h, 0, 0, 0:tokens, :]
        val = near[0, h, 1, 0, 0:tokens, :]
        queries = near[1, h, 0].reshape(6 * tokens, head_size)
        grads = near[1, h, 1].reshape(6 * tokens, head_size)
        scores = dot_nt(key, queries) * scale - stat_row(h)
        soft = jnp.exp(jnp.where(window(h), scores, masked_score))
        gv_ref[:, out_cols] = dot_nn(soft.astype(jnp.bfloat16), grads).astype(jnp.bfloat16)
        grad_scores = (soft * (dot_nt(val, grads) - stat_row(8 + h))).astype(jnp.bfloat16)
        gk_ref[:, out_cols] = (dot_nn(grad_scores, queries) * scale).astype(jnp.bfloat16)

    def stat_copies():
        targets = [
            (None, st_main.at[1], (pair, sp)),
            (has_other, st_main.at[2], (other, sp)),
        ]
        for slot, (cond, frame) in enumerate(((None, tm), (None, pair), (has_other, other))):
            for at, there, cond_s in ((st_down, sp - 1, has_up), (st_up, sp + 1, has_down)):
                both = cond_s if cond is None else cond & cond_s
                targets.append((both, at.at[slot], (frame, there)))
        arrivals = [None, has_other]
        for cond in (None, None, has_other):
            for cond_s in (has_down, has_up):
                arrivals.append(cond_s if cond is None else cond & cond_s)
        found = []
        for i, (cond, dst, device) in enumerate(targets):
            copy = pltpu.make_async_remote_copy(
                src_ref=st_main.at[0],
                dst_ref=dst,
                send_sem=stat_send.at[i],
                recv_sem=stat_recv.at[i],
                device_id=device,
                device_id_type=MESH,
            )
            found.append((cond, arrivals[i], copy))
        return found

    def when(cond, action):
        if cond is None:
            action()
        else:
            pl.when(cond)(action)

    stat_cols[...] = jnp.zeros_like(stat_cols)
    lag = 3
    slack = 2
    results = ((att_ref, att_out), (gq_ref, gq_out), (gk_ref, gk_out), (gv_ref, gv_out))

    def put(i, h):
        cols = slice(h * head_size, (h + 1) * head_size)
        return pltpu.make_async_copy(
            results[i][0].at[:, cols], results[i][1].at[:, cols], out_sem.at[i]
        )

    for h in range(head_count):
        load_wait(head_count + h)

    done = 0
    for j in range(count + lag):
        if j < count:
            pass_on(j)
        if j >= lag:
            pass_other(j - lag)
        if done < head_count and j >= min(done + lag + slack, count + lag - 1):
            last = head_count if j == count + lag - 1 else done + 1
            while done < last:
                if done == 0:
                    get_windows.wait()
                arrive_halo(done)
                forward(done)
                put(0, done).start()
                put(1, done).start()
                done += 1
            if done == head_count:
                st_main[0] = stat_cols[...].T[0:16, :]
                for cond, _, copy in stat_copies():
                    when(cond, copy.start)
    for _, cond, copy in stat_copies():
        when(cond, copy.wait_recv)
    for h in range(head_count):
        arrive_halo(head_count + h)
        backward(h)
        put(2, h).start()
        put(3, h).start()

    for cond, _, copy in stat_copies():
        when(cond, copy.wait_send)
    everything = near.at[:, :, :, 1, 0:tokens, :]
    remote(everything, everything, send_sem.at[0], recv_sem.at[0, 0], (pair, sp)).wait_send()
    when(
        has_to,
        remote(everything, everything, send_sem.at[1], recv_sem.at[0, 0], (pair, sp)).wait_send,
    )
    early = near.at[:, :, :, 0:2, 0:half, :]
    late = near.at[:, :, :, 2, 0:half, :]
    for i, cond in ((2, has_up), (4, has_down)):
        when(
            cond, remote(early, early, send_sem.at[i], recv_sem.at[0, 0], (pair, sp)).wait_send
        )
        when(
            cond & has_other,
            remote(late, late, send_sem.at[i + 1], recv_sem.at[0, 0], (pair, sp)).wait_send,
        )
    for i in range(4):
        pltpu.make_async_copy(results[i][0], results[i][1], out_sem.at[i]).wait()


def put_out(*refs):
    sources, targets, held, come, go = refs[:4], refs[4:8], refs[8], refs[9], refs[10]
    ins = [pltpu.make_async_copy(sources[i], held.at[i], come.at[i]) for i in range(4)]
    outs = [pltpu.make_async_copy(held.at[i], targets[i], go.at[i]) for i in range(4)]
    for copy in ins:
        copy.start()
    for i in range(4):
        ins[i].wait()
        outs[i].start()
    for copy in outs:
        copy.wait()


def on_device(queries, key_vectors, values, grad_out, windows):
    local_shape = queries.shape
    row_count, col_count, features = local_shape[1:]
    head_count = windows.shape[1]
    head_size = features // head_count
    tokens = row_count * col_count
    sizes = (
        head_count,
        head_size,
        row_count,
        col_count,
        lax.axis_size("tm"),
        lax.axis_size("space"),
    )
    flat = (tokens, features)
    count = 2 * head_count
    outs = pl.pallas_call(
        functools.partial(kernel, sizes),
        out_shape=[jax.ShapeDtypeStruct(flat, jnp.bfloat16)] * 4,
        in_specs=[pl.BlockSpec(memory_space=pl.ANY)] * 5,
        out_specs=[pl.BlockSpec(memory_space=pl.ANY)] * 4,
        scratch_shapes=[
            pltpu.SMEM((2, head_count), jnp.int32),
            pltpu.VMEM(flat, jnp.bfloat16),
            pltpu.VMEM(flat, jnp.bfloat16),
            pltpu.VMEM(flat, jnp.bfloat16),
            pltpu.VMEM(flat, jnp.bfloat16),
            pltpu.VMEM((2, head_count, 2, 3, 2 * tokens, head_size), jnp.bfloat16),
            pltpu.VMEM((tokens, tokens), jnp.float32),
            pltpu.VMEM((3, 16, tokens), jnp.float32),
            pltpu.VMEM((3, 16, tokens), jnp.float32),
            pltpu.VMEM((3, 16, tokens), jnp.float32),
            pltpu.SemaphoreType.DMA((count + 1,)),
            pltpu.SemaphoreType.DMA((6,)),
            pltpu.SemaphoreType.DMA((count, 6)),
            pltpu.SemaphoreType.DMA((8,)),
            pltpu.SemaphoreType.DMA((8,)),
            pltpu.SemaphoreType.DMA((4,)),
        ],
        compiler_params=pltpu.CompilerParams(
            collective_id=0, has_side_effects=True, vmem_limit_bytes=63_000_000
        ),
    )(
        windows,
        queries.reshape(flat),
        key_vectors.reshape(flat),
        values.reshape(flat),
        grad_out.reshape(flat),
    )
    outs = pl.pallas_call(
        put_out,
        out_shape=[jax.ShapeDtypeStruct(flat, jnp.bfloat16)] * 4,
        in_specs=[pl.BlockSpec(memory_space=pl.ANY)] * 4,
        out_specs=[pl.BlockSpec(memory_space=pl.ANY)] * 4,
        scratch_shapes=[
            pltpu.VMEM((4,) + flat, jnp.bfloat16),
            pltpu.SemaphoreType.DMA((4,)),
            pltpu.SemaphoreType.DMA((4,)),
        ],
        compiler_params=pltpu.CompilerParams(vmem_limit_bytes=63_000_000),
    )(*outs)
    return tuple(out.reshape(local_shape) for out in outs)


def solution(mesh):
    spec = P("tm", "space", None, None)
    return jax.shard_map(
        on_device,
        mesh=mesh,
        in_specs=(spec, spec, spec, spec, P()),
        out_specs=(spec, spec, spec, spec),
        check_vma=False,
    )
```

```python
import functools
import math

import jax
import jax.numpy as jnp
from jax import lax
from jax.experimental import pallas as pl
from jax.experimental.pallas import tpu as pltpu
from jax.sharding import PartitionSpec as P

masked_score = -1e30
MESH = pl.DeviceIdType.MESH


def dot_nt(a, b):
    return lax.dot_general(a, b, (((1,), (1,)), ((), ())), preferred_element_type=jnp.float32)


def dot_nn(a, b):
    return lax.dot_general(a, b, (((1,), (0,)), ((), ())), preferred_element_type=jnp.float32)


def kernel(
    sizes,
    win_hbm,
    q_ref,
    k_ref,
    v_ref,
    g_ref,
    att_ref,
    gq_ref,
    gk_ref,
    gv_ref,
    win_ref,
    near,
    stat_cols,
    st_main,
    st_down,
    st_up,
    load_sem,
    send_sem,
    recv_sem,
    stat_send,
    stat_recv,
):
    head_count, head_size, row_count, col_count, n_tm, n_space = sizes
    tokens = row_count * col_count
    half = tokens // 2
    scale = 1.0 / math.sqrt(head_size)
    tm, sp = lax.axis_index("tm"), lax.axis_index("space")
    side = lax.rem(tm, 2)
    pair = tm + 1 - 2 * side
    other = tm - 1 + 2 * side
    relay_to = tm + 2 - 4 * side
    relay_from = tm - 2 + 4 * side
    has_other = (other >= 0) & (other < n_tm)
    has_to = (relay_to >= 0) & (relay_to < n_tm)
    has_from = (relay_from >= 0) & (relay_from < n_tm)
    has_up = sp > 0
    has_down = sp < n_space - 1

    st_main[...] = jnp.zeros_like(st_main)
    st_down[...] = jnp.zeros_like(st_down)
    st_up[...] = jnp.zeros_like(st_up)

    barrier = pltpu.get_barrier_semaphore()

    def greet(cond, tm_to, sp_to):
        @pl.when(cond)
        def _():
            pl.semaphore_signal(barrier, inc=1, device_id=(tm_to, sp_to), device_id_type=MESH)

    pl.semaphore_signal(barrier, inc=1, device_id=(pair, sp), device_id_type=MESH)
    greet(has_to, relay_to, sp)
    greet(has_from, relay_from, sp)
    greet(has_up, tm, sp - 1)
    greet(has_down, tm, sp + 1)

    near_arrays = ((k_ref, v_ref), (q_ref, g_ref))
    pieces = [(phase, h) for phase in range(2) for h in range(head_count)]
    count = len(pieces)

    def block(j, slot, start, size):
        phase, h = pieces[j]
        return near.at[phase, h, :, slot, start : start + size, :]

    def source(j, a):
        phase, h = pieces[j]
        return near_arrays[phase][a].at[:, h * head_size : (h + 1) * head_size]

    def load(j, a):
        phase, h = pieces[j]
        return pltpu.make_async_copy(
            source(j, a), near.at[phase, h, a, 0, 0:tokens, :], load_sem.at[j]
        )

    def load_wait(j):
        whole = block(j, 0, 0, tokens)
        pltpu.make_async_copy(whole, whole, load_sem.at[j]).wait()

    def remote(src, dst, send, recv, device):
        return pltpu.make_async_remote_copy(
            src_ref=src,
            dst_ref=dst,
            send_sem=send,
            recv_sem=recv,
            device_id=device,
            device_id_type=MESH,
        )

    def to_pair(j, a):
        phase, h = pieces[j]
        return remote(
            source(j, a),
            near.at[phase, h, a, 1, 0:tokens, :],
            send_sem.at[0],
            recv_sem.at[j, 0],
            (pair, sp),
        )

    def both_pair(j):
        whole = block(j, 1, 0, tokens)
        return remote(whole, whole, send_sem.at[0], recv_sem.at[j, 0], (pair, sp))

    def to_relay(j):
        return remote(
            block(j, 1, 0, tokens),
            block(j, 2, 0, tokens),
            send_sem.at[1],
            recv_sem.at[j, 1],
            (relay_to, sp),
        )

    def to_up(j, slot, size=None):
        slots = slot if size is None else slice(slot, slot + size)
        late = 1 if slot == 2 else 0
        return remote(
            block(j, slots, 0, half),
            block(j, slots, tokens, half),
            send_sem.at[2 + late],
            recv_sem.at[j, 2 + late],
            (tm, sp - 1),
        )

    def to_down(j, slot, size=None):
        slots = slot if size is None else slice(slot, slot + size)
        late = 1 if slot == 2 else 0
        return remote(
            block(j, slots, half, half),
            block(j, slots, tokens + half, half),
            send_sem.at[4 + late],
            recv_sem.at[j, 4 + late],
            (tm, sp + 1),
        )

    def rows_out(j, slot):
        @pl.when(has_up)
        def _():
            to_up(j, slot).start()

        @pl.when(has_down)
        def _():
            to_down(j, slot).start()

    def pass_on(j):
        if pieces[j][0] == 0:
            load_wait(j)
        rows_out(j, 0)
        both_pair(j).wait_recv()

        @pl.when(has_to)
        def _():
            to_relay(j).start()

        rows_out(j, 1)

    def pass_other(j):
        @pl.when(has_other)
        def _():
            to_relay(j).wait_recv()
            rows_out(j, 2)

    def arrive_halo(j):
        @pl.when(has_down)
        def _():
            to_up(j, 0, 2).wait_recv()

        @pl.when(has_up)
        def _():
            to_down(j, 0, 2).wait_recv()

        @pl.when(has_down & has_other)
        def _():
            to_up(j, 2).wait_recv()

        @pl.when(has_up & has_other)
        def _():
            to_down(j, 2).wait_recv()

    get_windows = pltpu.make_async_copy(win_hbm, win_ref, load_sem.at[count])
    get_windows.start()
    for j in range(count):
        for a in range(2):
            load(j, a).start()

    expected = (
        1
        + has_to.astype(jnp.int32)
        + has_from.astype(jnp.int32)
        + has_up.astype(jnp.int32)
        + has_down.astype(jnp.int32)
    )
    pl.semaphore_wait(barrier, expected)
    for j in range(count):
        for a in range(2):
            to_pair(j, a).start()

    @pl.when(jnp.logical_not(has_other))
    def _():
        for phase, h in pieces:
            near[phase, h, :, 2] = jnp.zeros((2, 2 * tokens, head_size), near.dtype)

    @pl.when(jnp.logical_not(has_down))
    def _():
        for phase, h in pieces:
            near[phase, h, :, :, tokens : tokens + half, :] = jnp.zeros(
                (2, 3, half, head_size), near.dtype
            )

    @pl.when(jnp.logical_not(has_up))
    def _():
        for phase, h in pieces:
            near[phase, h, :, :, tokens + half : 2 * tokens, :] = jnp.zeros(
                (2, 3, half, head_size), near.dtype
            )

    own_id = lax.broadcasted_iota(jnp.int32, (tokens, 2 * tokens), 0)
    near_id = lax.broadcasted_iota(jnp.int32, (tokens, 2 * tokens), 1)
    own_row, own_col = own_id // col_count, own_id % col_count
    near_row, near_col = near_id // col_count, near_id % col_count
    upper = near_row >= row_count + row_count // 2
    near_row = jnp.where(upper, near_row - 2 * row_count, near_row)
    global_row = sp * row_count + near_row
    row_inside = (global_row >= 0) & (global_row < n_space * row_count)
    row_gap = jnp.where(row_inside, jnp.abs(own_row - near_row), 1 << 20)
    col_gap = jnp.abs(own_col - near_col)
    other_gap = jnp.where(has_other, 0, 1 << 20)

    def window(h):
        col_in = col_gap <= win_ref[1, h]
        here = (row_gap <= win_ref[0, h]) & col_in
        there = (row_gap + other_gap <= win_ref[0, h]) & col_in
        return jnp.concatenate([here, here, there], axis=1)

    lane = lax.broadcasted_iota(jnp.int32, (tokens, tokens), 1)

    def forward(h):
        out_cols = slice(h * head_size, (h + 1) * head_size)
        query = near[1, h, 0, 0, 0:tokens, :]
        grad = near[1, h, 1, 0, 0:tokens, :]
        keys = near[0, h, 0].reshape(6 * tokens, head_size)
        vals = near[0, h, 1].reshape(6 * tokens, head_size)
        scores = jnp.where(window(h), dot_nt(query, keys) * scale, masked_score)
        top = jnp.max(scores, axis=1, keepdims=True)
        powers = jnp.exp(scores - top)
        total = jnp.sum(powers, axis=1, keepdims=True)
        soft = powers * (1.0 / total)
        attended = dot_nn(soft.astype(jnp.bfloat16), vals).astype(jnp.bfloat16)
        att_ref[:, out_cols] = attended
        out_dot = jnp.sum(
            grad.astype(jnp.float32) * attended.astype(jnp.float32), axis=1, keepdims=True
        )
        grad_scores = (soft * (dot_nt(grad, vals) - out_dot)).astype(jnp.bfloat16)
        gq_ref[:, out_cols] = (dot_nn(grad_scores, keys) * scale).astype(jnp.bfloat16)
        log_total = top + jnp.log(total)
        stats = jnp.where(lane == h, log_total, stat_cols[...])
        stat_cols[...] = jnp.where(lane == 8 + h, out_dot, stats)

    row_lane = lax.broadcasted_iota(jnp.int32, (1, tokens), 1)

    def stat_row(r):
        parts = []
        for slot in range(3):
            parts.append(st_main[slot, r : r + 1, :])
            parts.append(
                jnp.where(row_lane < half, st_down[slot, r : r + 1, :], st_up[slot, r : r + 1, :])
            )
        return jnp.concatenate(parts, axis=1)

    def backward(h):
        out_cols = slice(h * head_size, (h + 1) * head_size)
        key = near[0, h, 0, 0, 0:tokens, :]
        val = near[0, h, 1, 0, 0:tokens, :]
        queries = near[1, h, 0].reshape(6 * tokens, head_size)
        grads = near[1, h, 1].reshape(6 * tokens, head_size)
        scores = dot_nt(key, queries) * scale - stat_row(h)
        soft = jnp.exp(jnp.where(window(h), scores, masked_score))
        gv_ref[:, out_cols] = dot_nn(soft.astype(jnp.bfloat16), grads).astype(jnp.bfloat16)
        grad_scores = (soft * (dot_nt(val, grads) - stat_row(8 + h))).astype(jnp.bfloat16)
        gk_ref[:, out_cols] = (dot_nn(grad_scores, queries) * scale).astype(jnp.bfloat16)

    def stat_copies():
        targets = [
            (None, st_main.at[1], (pair, sp)),
            (has_other, st_main.at[2], (other, sp)),
        ]
        for slot, (cond, frame) in enumerate(((None, tm), (None, pair), (has_other, other))):
            for at, there, cond_s in ((st_down, sp - 1, has_up), (st_up, sp + 1, has_down)):
                both = cond_s if cond is None else cond & cond_s
                targets.append((both, at.at[slot], (frame, there)))
        arrivals = [None, has_other]
        for cond in (None, None, has_other):
            for cond_s in (has_down, has_up):
                arrivals.append(cond_s if cond is None else cond & cond_s)
        found = []
        for i, (cond, dst, device) in enumerate(targets):
            copy = pltpu.make_async_remote_copy(
                src_ref=st_main.at[0],
                dst_ref=dst,
                send_sem=stat_send.at[i],
                recv_sem=stat_recv.at[i],
                device_id=device,
                device_id_type=MESH,
            )
            found.append((cond, arrivals[i], copy))
        return found

    def when(cond, action):
        if cond is None:
            action()
        else:
            pl.when(cond)(action)

    stat_cols[...] = jnp.zeros_like(stat_cols)
    lag = 3
    slack = 2
    for h in range(head_count):
        load_wait(head_count + h)

    done = 0
    for j in range(count + lag):
        if j < count:
            pass_on(j)
        if j >= lag:
            pass_other(j - lag)
        if done < head_count and j >= min(done + lag + slack, count + lag - 1):
            last = head_count if j == count + lag - 1 else done + 1
            while done < last:
                if done == 0:
                    get_windows.wait()
                arrive_halo(done)
                forward(done)
                done += 1
            if done == head_count:
                st_main[0] = stat_cols[...].T[0:16, :]
                for cond, _, copy in stat_copies():
                    when(cond, copy.start)
    for _, cond, copy in stat_copies():
        when(cond, copy.wait_recv)
    for h in range(head_count):
        arrive_halo(head_count + h)
        backward(h)

    for cond, _, copy in stat_copies():
        when(cond, copy.wait_send)
    everything = near.at[:, :, :, 1, 0:tokens, :]
    remote(everything, everything, send_sem.at[0], recv_sem.at[0, 0], (pair, sp)).wait_send()
    when(
        has_to,
        remote(everything, everything, send_sem.at[1], recv_sem.at[0, 0], (pair, sp)).wait_send,
    )
    early = near.at[:, :, :, 0:2, 0:half, :]
    late = near.at[:, :, :, 2, 0:half, :]
    for i, cond in ((2, has_up), (4, has_down)):
        when(
            cond, remote(early, early, send_sem.at[i], recv_sem.at[0, 0], (pair, sp)).wait_send
        )
        when(
            cond & has_other,
            remote(late, late, send_sem.at[i + 1], recv_sem.at[0, 0], (pair, sp)).wait_send,
        )


def put_out(*refs):
    sources, targets, sems = refs[:4], refs[4:8], refs[8]
    copies = [pltpu.make_async_copy(sources[i], targets[i], sems.at[i]) for i in range(4)]
    for copy in copies:
        copy.start()
    for copy in copies:
        copy.wait()


def on_device(queries, key_vectors, values, grad_out, windows):
    local_shape = queries.shape
    row_count, col_count, features = local_shape[1:]
    head_count = windows.shape[1]
    head_size = features // head_count
    tokens = row_count * col_count
    sizes = (
        head_count,
        head_size,
        row_count,
        col_count,
        lax.axis_size("tm"),
        lax.axis_size("space"),
    )
    flat = (tokens, features)
    count = 2 * head_count
    outs = pl.pallas_call(
        functools.partial(kernel, sizes),
        out_shape=[jax.ShapeDtypeStruct(flat, jnp.bfloat16)] * 4,
        in_specs=[pl.BlockSpec(memory_space=pl.ANY)] * 5,
        out_specs=[pl.BlockSpec(memory_space=pltpu.VMEM)] * 4,
        scratch_shapes=[
            pltpu.SMEM((2, head_count), jnp.int32),
            pltpu.VMEM((2, head_count, 2, 3, 2 * tokens, head_size), jnp.bfloat16),
            pltpu.VMEM((tokens, tokens), jnp.float32),
            pltpu.VMEM((3, 16, tokens), jnp.float32),
            pltpu.VMEM((3, 16, tokens), jnp.float32),
            pltpu.VMEM((3, 16, tokens), jnp.float32),
            pltpu.SemaphoreType.DMA((count + 1,)),
            pltpu.SemaphoreType.DMA((6,)),
            pltpu.SemaphoreType.DMA((count, 6)),
            pltpu.SemaphoreType.DMA((8,)),
            pltpu.SemaphoreType.DMA((8,)),
        ],
        compiler_params=pltpu.CompilerParams(
            collective_id=0, has_side_effects=True, vmem_limit_bytes=55_600_000
        ),
    )(
        windows,
        queries.reshape(flat),
        key_vectors.reshape(flat),
        values.reshape(flat),
        grad_out.reshape(flat),
    )
    outs = pl.pallas_call(
        put_out,
        out_shape=[jax.ShapeDtypeStruct(flat, jnp.bfloat16)] * 4,
        in_specs=[pl.BlockSpec(memory_space=pltpu.VMEM)] * 4,
        out_specs=[pl.BlockSpec(memory_space=pltpu.HBM)] * 4,
        scratch_shapes=[
            pltpu.SemaphoreType.DMA((4,)),
        ],
        compiler_params=pltpu.CompilerParams(vmem_limit_bytes=4_000_000),
    )(*outs)
    return tuple(out.reshape(local_shape) for out in outs)


def solution(mesh):
    spec = P("tm", "space", None, None)
    return jax.shard_map(
        on_device,
        mesh=mesh,
        in_specs=(spec, spec, spec, spec, P()),
        out_specs=(spec, spec, spec, spec),
        check_vma=False,
    )
```
